1024 devices in a mesh: grp: 16 (over z_lo, core), dev: 64 (over y, x, z_hi).
Axes of the slice: x: 4, y: 4, z: 32 (z_hi: 4, z_lo: 8; z = z_hi * 8 + z_lo), core: 2. Of those that a mesh axis runs over, the one named last changes fastest.
Arguments:
- amplitudes: float32 [2, 65536, 128], P(None, ('grp', 'dev')), may hold values from -6 to 6
- couplings: float32 [2, 12, 128, 128], replicated, may hold values from -1 to 1, as said below
- block_index: int32 [4096], P(('grp', 'dev')), may hold values from 0 to 11
- bond_map: int32 [10], replicated, may hold values from 0 to 6
- bond_strength: float32 [10], replicated, may hold values from 0.05 to 0.5
- drive_amplitude: float32 [4, 10], replicated, may hold values from 0.05 to 0.5
Outputs:
- new_amplitudes: float32 [2, 65536, 128], P(None, ('grp', 'dev'))
The draws below stay inside these ranges and needn't reach their ends.
Inputs may be any that keep to these rules, and one draw needn't show every extreme that they name: couplings[0][k] is symmetric and couplings[1][k] antisymmetric, so each listed coupling is Hermitian.
All inputs are finite; a program needn't handle non-finite values.
Results may differ from the reference program's by a relative error of at most 0.00007.
Values sent between devices are 32-bit elements; how exact they have to be, the bound alone decides.
No kernel may reach another device: no remote copies, remote signals or barrier semaphores. Data moves between devices by JAX's collectives and lax.ppermute only.
A program may use at most 32 MiB of HBM per device.

```python
import math
import jax
import jax.numpy as jnp
from jax import lax

COLS = 128
KINDS = 12
BROWS = 16
SECTIONS = 4
ROWS = 64
COL_SPINS = 7
LEAD = 10
NBLK = 4
TOTAL_ROWS = 65536
TOTAL_BLOCKS = 4096


def draw_couplings(key, part):
    first_key, second_key = jax.random.split(jax.random.fold_in(key, 7))
    shape = (KINDS, COLS, COLS)
    sym_base = jax.random.uniform(first_key, shape, jnp.float32, -1.0, 1.0)
    anti_base = jax.random.uniform(second_key, shape, jnp.float32, -1.0, 1.0)
    scale = 1.2 / COLS ** 0.5
    real_block = 0.5 * scale * (sym_base + jnp.swapaxes(sym_base, 1, 2))
    imag_block = 0.5 * scale * (anti_base - jnp.swapaxes(anti_base, 1, 2))
    return jnp.stack([real_block, imag_block]).astype(jnp.float32)


def plant(entries, own_key, low, top_value):
    shape = entries.shape
    spot = [jax.random.randint(jax.random.fold_in(own_key, axis), (), 0, shape[axis]) for axis in range(len(shape))]
    entries = entries.at[tuple(spot)].set(low)
    longest = shape.index(max(shape))
    spot[longest] = (spot[longest] + 1) % shape[longest]
    return entries.at[tuple(spot)].set(top_value)


def block_levels(rng, shape, cuts, low, top_value):
    loudness = 1.0
    for axis_at, parts in cuts:
        steps = jax.random.uniform(jax.random.fold_in(jax.random.fold_in(rng, 6), axis_at), (parts,), jnp.float32, low / len(cuts), top_value / len(cuts))
        loudness = loudness * jnp.repeat(jnp.exp(steps), shape[axis_at] // parts).reshape((-1,) + (1,) * (len(shape) - 1 - axis_at))
    return loudness


def normal_values(stream_key, extent, width, reach, shards=(), held_as=jnp.bfloat16):
    values = width * jax.random.normal(stream_key, extent, jnp.float32)
    if shards:
        values = values * block_levels(stream_key, extent, shards, -0.22, 0.18)
    return jnp.clip(values, -reach, reach).astype(held_as)


def setup_inputs(seed: int = 0) -> dict:
    keys = jax.random.split(jax.random.key(seed), 7)
    amplitudes = normal_values(keys[0], (2, TOTAL_ROWS, COLS), 1.0, 6.0, ((1, 1024),), jnp.float32)
    couplings = draw_couplings(jax.random.fold_in(keys[6], 71), 0)
    block_index = plant(jax.random.randint(keys[2], (TOTAL_BLOCKS,), 0, KINDS), jax.random.fold_in(keys[2], 1), 0, KINDS - 1).astype(jnp.int32)
    bond_map = plant(jax.random.randint(keys[3], (LEAD,), 0, COL_SPINS), jax.random.fold_in(keys[3], 1), 0, COL_SPINS - 1).astype(jnp.int32)
    bond_strength = jnp.clip(jnp.exp(jax.random.uniform(keys[4], (LEAD,), jnp.float32, math.log(0.05), math.log(0.5))), 0.05, 0.5)
    drive_amplitude = jnp.clip(jnp.exp(jax.random.uniform(keys[5], (SECTIONS, LEAD), jnp.float32, math.log(0.05), math.log(0.5))), 0.05, 0.5)
    return {"amplitudes": amplitudes, "couplings": couplings, "block_index": block_index, "bond_map": bond_map, "bond_strength": bond_strength, "drive_amplitude": drive_amplitude}


STEP_SIZE = 0.5
HIGHEST = lax.Precision.HIGHEST


def coupled(real_part, imag_part, couplings, block_index):
    dev_total = TOTAL_ROWS // ROWS
    real_four = real_part.reshape(dev_total, NBLK, BROWS, COLS)
    imag_four = imag_part.reshape(dev_total, NBLK, BROWS, COLS)
    kind_rows = block_index.reshape(dev_total, NBLK)

    def one_device(items):
        block_real, block_imag, kind_now = items
        mat_real = jnp.take(couplings[0], kind_now, axis=0)
        mat_imag = jnp.take(couplings[1], kind_now, axis=0)

        def apply_mat(field, matrix):
            return jnp.einsum("brj,bcj->brc", field, matrix, precision=HIGHEST)

        out_real = apply_mat(block_real, mat_real) - apply_mat(block_imag, mat_imag)
        out_imag = apply_mat(block_imag, mat_real) + apply_mat(block_real, mat_imag)
        return out_real, out_imag

    out_real, out_imag = lax.map(one_device, (real_four, imag_four, kind_rows))
    return out_real.reshape(TOTAL_ROWS, COLS), out_imag.reshape(TOTAL_ROWS, COLS)


def flip_leading(field, lead_spin):
    outer_count = TOTAL_ROWS // (ROWS * 2 ** (lead_spin + 1))
    folded = field.reshape(outer_count, 2, ROWS * 2 ** lead_spin, COLS)
    return folded[:, ::-1].reshape(TOTAL_ROWS, COLS)


def evaluate_field(real_part, imag_part, couplings, block_index, bond_map, bond_strength, drive_row):
    out_real, out_imag = coupled(real_part, imag_part, couplings, block_index)
    columns = jnp.arange(COLS, dtype=jnp.int32)
    devices = jnp.arange(TOTAL_ROWS, dtype=jnp.int32) // ROWS
    for lead_spin in range(LEAD):
        target = bond_map[lead_spin]
        shuffle = jnp.bitwise_xor(columns, jnp.left_shift(jnp.int32(1), target)).astype(jnp.int32)
        sign_col = (1 - 2 * jnp.bitwise_and(jnp.right_shift(columns, target), 1)).astype(jnp.float32)[None, :]
        sign_lead = (1 - 2 * jnp.bitwise_and(jnp.right_shift(devices, lead_spin), 1)).astype(jnp.float32)[:, None]
        part_real = flip_leading(real_part, lead_spin)
        part_imag = flip_leading(imag_part, lead_spin)
        strength = bond_strength[lead_spin]
        drive_now = drive_row[lead_spin]
        out_real = out_real + strength * (sign_lead * sign_col * real_part + jnp.take(part_real, shuffle, axis=1)) + drive_now * part_real
        out_imag = out_imag + strength * (sign_lead * sign_col * imag_part + jnp.take(part_imag, shuffle, axis=1)) + drive_now * part_imag
    return out_imag, -out_real


def runge_kutta(real_part, imag_part, evaluate):
    half_step = 0.5 * STEP_SIZE
    slope_one = evaluate(0, real_part, imag_part)
    slope_two = evaluate(1, real_part + half_step * slope_one[0], imag_part + half_step * slope_one[1])
    slope_three = evaluate(2, real_part + half_step * slope_two[0], imag_part + half_step * slope_two[1])
    slope_four = evaluate(3, real_part + STEP_SIZE * slope_three[0], imag_part + STEP_SIZE * slope_three[1])
    factor = STEP_SIZE / 6.0
    new_real = real_part + factor * (slope_one[0] + 2.0 * slope_two[0] + 2.0 * slope_three[0] + slope_four[0])
    new_imag = imag_part + factor * (slope_one[1] + 2.0 * slope_two[1] + 2.0 * slope_three[1] + slope_four[1])
    return new_real, new_imag


def reference(amplitudes, couplings, block_index, bond_map, bond_strength, drive_amplitude):
    def evaluate(section, first, second):
        return evaluate_field(first, second, couplings, block_index, bond_map, bond_strength, drive_amplitude[section])

    new_real, new_imag = runge_kutta(amplitudes[0], amplitudes[1], evaluate)
    return jnp.stack([new_real, new_imag])
```

```python
import functools

import jax
import jax.numpy as jnp
from jax import lax
from jax.experimental import pallas as pl
from jax.experimental.pallas import tpu as pltpu
from jax.sharding import Mesh, PartitionSpec as P

BROWS = 16
STEP_SIZE = 0.5

ROWS = 64
COLS = 128
KINDS = 12
LEAD = 10
UNITS = 16
PAYLOAD = 136
TWO = 2 * COLS

ORDER = sorted(range(UNITS), key=lambda u: (u.bit_count(), u))
PLANE = {2: 0, 3: 1, 4: 2, 5: 3}
ROW_BIT = {0: 0, 1: 1, 6: 2, 7: 3, 8: 4, 9: 5}
GROUPS = ((5, 5, 5), (6, 5), (5,), (1,))


def prep_kernel(index_ref, amp_ref, out_ref):
    out_ref[:, 0, 0:COLS] = amp_ref[0]
    out_ref[:, 0, COLS:TWO] = amp_ref[1]
    block = lax.broadcasted_iota(jnp.int32, (ROWS, COLS), 0) // BROWS
    kind = jnp.zeros((ROWS, COLS), jnp.int32)
    for q in range(ROWS // BROWS):
        kind = jnp.where(block == q, index_ref[q], kind)
    out_ref[:, 0, TWO : TWO + COLS] = kind.astype(jnp.float32)


def pack_kernel(in_ref, out_ref):
    real = in_ref[:, 0, 0:COLS]
    imag = in_ref[:, 0, COLS:TWO]
    kind = in_ref[:, 0, TWO : TWO + COLS]
    row = lax.broadcasted_iota(jnp.int32, (ROWS, COLS), 0)
    lane = lax.broadcasted_iota(jnp.int32, (ROWS, COLS), 1)
    kinds = jnp.sum(jnp.where(row == lane, kind, 0.0), axis=0, keepdims=True)
    kinds = jnp.broadcast_to(kinds, (PAYLOAD - 2 * ROWS, COLS))
    for u in range(UNITS):
        out_ref[u, 0:ROWS] = real
        out_ref[u, ROWS : 2 * ROWS] = imag
        out_ref[u, 2 * ROWS :] = kinds


def unpack_kernel(in_ref, out_ref):
    out_ref[0] = in_ref[:, 0, 0:COLS]
    out_ref[1] = in_ref[:, 0, COLS:TWO]


def flip_rows(field, bit):
    if bit >= 3:
        step = 1 << (bit - 3)
        tiles = field.reshape(8 // (2 * step), 2, step, 8, COLS)
        return jnp.concatenate([tiles[:, 1:], tiles[:, :1]], axis=1).reshape(ROWS, COLS)
    tiles = field.reshape(8, 8, COLS)
    step = 1 << bit
    if bit == 2:
        return pltpu.roll(tiles, 4, 1).reshape(ROWS, COLS)
    row = lax.broadcasted_iota(jnp.int32, (8, 8, COLS), 1)
    up = pltpu.roll(tiles, 8 - step, 1)
    down = pltpu.roll(tiles, step, 1)
    return jnp.where((row & step) == 0, up, down).reshape(ROWS, COLS)


def step_kernel(
    bond_ref,
    strength_ref,
    drive_ref,
    gathered_ref,
    couplings_ref,
    out_ref,
    order_ref,
    states,
    kinds,
    diag_ref,
    sign_ref,
    lane_ref,
    high_w,
    low_w,
    high_x,
    low_x,
    lead_ref,
    total,
):
    own = lax.axis_index("plane")
    for p, u in enumerate(ORDER):
        order_ref[p] = jnp.int32(u)

    def split(k, carry):
        real = couplings_ref[0, k]
        imag = couplings_ref[1, k]
        for r, row in enumerate(((real, -imag), (imag, real))):
            for c, block in enumerate(row):
                rows = pl.ds(pl.multiple_of(k * TWO + r * COLS, COLS), COLS)
                high = block.astype(jnp.bfloat16)
                high_w[rows, c * COLS : (c + 1) * COLS] = high
                low_w[rows, c * COLS : (c + 1) * COLS] = (
                    block - high.astype(jnp.float32)
                ).astype(jnp.bfloat16)
        return carry

    lax.fori_loop(0, KINDS, split, 0)

    row = lax.broadcasted_iota(jnp.int32, (ROWS, COLS), 0)
    lane = lax.broadcasted_iota(jnp.int32, (ROWS, COLS), 1)

    diag = jnp.zeros((ROWS, COLS), jnp.float32)
    for a in range(LEAD):
        target = bond_ref[a]
        lane_ref[a] = jnp.bitwise_xor(lane[:8], jnp.left_shift(jnp.int32(1), target))
        sign = (1 - 2 * jnp.bitwise_and(jnp.right_shift(lane, target), 1)).astype(jnp.float32)
        sign = strength_ref[a] * sign
        if a in PLANE:
            sign_ref[PLANE[a]] = sign[:8]
        else:
            lead = (1 - 2 * jnp.bitwise_and(jnp.right_shift(row, ROW_BIT[a]), 1)).astype(jnp.float32)
            diag = diag + lead * sign
    diag_ref[...] = diag

    def arrive(u, carry):
        there = jnp.bitwise_xor(u, own)
        states[0, u, 0] = gathered_ref[there, 0:ROWS]
        states[0, u, 1] = gathered_ref[there, ROWS : 2 * ROWS]
        listed = jnp.broadcast_to(gathered_ref[there, 2 * ROWS : 2 * ROWS + 1], (ROWS, COLS))
        kind = jnp.sum(jnp.where(row == lane, listed, 0.0), axis=1, keepdims=True)
        kinds[u] = jnp.broadcast_to(kind, (ROWS, COLS)).astype(jnp.bfloat16)
        return carry

    lax.fori_loop(0, UNITS, arrive, 0)

    def scatter(section, p):
        u = order_ref[p]
        rows = pl.ds(pl.multiple_of(p * ROWS, ROWS), ROWS)
        kind = kinds[u]
        for part in range(2):
            x = states[section, u, part]
            high = x.astype(jnp.bfloat16)
            low = (x - high.astype(jnp.float32)).astype(jnp.bfloat16)
            zero = jnp.zeros_like(high)
            for k in range(KINDS):
                chosen = kind == jnp.bfloat16(k)
                at = k * TWO + part * COLS
                high_x[rows, at : at + COLS] = jnp.where(chosen, high, zero)
                low_x[rows, at : at + COLS] = jnp.where(chosen, low, zero)
        weight = jnp.zeros((8, COLS), jnp.float32)
        here = jnp.bitwise_xor(u, own)
        for bit in range(4):
            sign = (1 - 2 * jnp.bitwise_and(jnp.right_shift(here, bit), 1)).astype(jnp.float32)
            weight = weight + sign * sign_ref[bit]
        weight = (diag_ref[...].reshape(8, 8, COLS) + weight[None]).reshape(ROWS, COLS)
        for part in range(2):
            x = states[section, u, part]
            out = weight * x
            for a in range(LEAD):
                if a in PLANE:
                    y = states[section, jnp.bitwise_xor(u, 1 << PLANE[a]), part]
                else:
                    y = x
                where = jnp.broadcast_to(lane_ref[a][None], (8, 8, COLS)).reshape(ROWS, COLS)
                shuffled = jnp.take_along_axis(y, where, axis=1)
                term = strength_ref[a] * shuffled + drive_ref[section, a] * y
                if a not in PLANE:
                    term = flip_rows(term, ROW_BIT[a])
                out = out + term
            lead_ref[p, part] = out

    def combine(section, first, count):
        rows = pl.ds(pl.multiple_of(first * ROWS, ROWS), count * ROWS)
        dot = functools.partial(jnp.dot, preferred_element_type=jnp.float32)
        out = dot(high_x[rows, :], high_w[...])
        out = out + dot(low_x[rows, :], high_w[...])
        out = out + dot(high_x[rows, :], low_w[...])
        ahead = (0.5, 0.5, 1.0, 0.0)[section] * STEP_SIZE
        for i in range(count):
            u = order_ref[first + i]
            h_real = out[i * ROWS : (i + 1) * ROWS, :COLS] + lead_ref[first + i, 0]
            h_imag = out[i * ROWS : (i + 1) * ROWS, COLS:] + lead_ref[first + i, 1]
            if section < 3:
                states[section + 1, u, 0] = states[0, u, 0] + ahead * h_imag
                states[section + 1, u, 1] = states[0, u, 1] - ahead * h_real
            if i == 0:
                share = (1.0, 2.0, 2.0, 1.0)[section] * STEP_SIZE / 6.0

                def keep():
                    if section == 0:
                        total[0] = states[0, 0, 0] + share * h_imag
                        total[1] = states[0, 0, 1] - share * h_real
                    elif section < 3:
                        total[0] = total[0] + share * h_imag
                        total[1] = total[1] - share * h_real
                    else:
                        out_ref[:, 0, 0:COLS] = total[0] + share * h_imag
                        out_ref[:, 0, COLS:TWO] = total[1] - share * h_real

                if isinstance(first, int):
                    if first == 0:
                        keep()
                else:
                    pl.when(first == 0)(keep)

    for section, groups in enumerate(GROUPS):

        def one(p, carry, section=section):
            scatter(section, p)
            return carry

        lax.fori_loop(0, sum(groups), one, 0)
        if len(set(groups)) == 1 and len(groups) > 1:

            def many(c, carry, section=section, count=groups[0]):
                combine(section, c * count, count)
                return carry

            lax.fori_loop(0, len(groups), many, 0)
        else:
            first = 0
            for count in groups:
                combine(section, first, count)
                first += count


def body(amplitudes, couplings, block_index, bond_map, bond_strength, drive_amplitude):
    f32 = jnp.float32
    vmem = pl.BlockSpec(memory_space=pltpu.VMEM)
    smem = pl.BlockSpec(memory_space=pltpu.SMEM)
    line = ("grp", "far")
    sent = pl.pallas_call(
        prep_kernel,
        out_shape=jax.ShapeDtypeStruct((ROWS, 1, TWO + COLS), f32),
        in_specs=[smem, vmem],
        out_specs=vmem,
    )(block_index, amplitudes)
    held = lax.all_to_all(sent, line, 0, 0, tiled=True)
    copies = pl.pallas_call(
        pack_kernel,
        out_shape=jax.ShapeDtypeStruct((UNITS, PAYLOAD, COLS), f32),
        in_specs=[vmem],
        out_specs=vmem,
    )(held)
    gathered = lax.all_to_all(copies, "plane", 0, 0, tiled=True)
    result = pl.pallas_call(
        step_kernel,
        out_shape=jax.ShapeDtypeStruct((ROWS, 1, TWO), f32),
        in_specs=[smem, smem, smem, vmem, vmem],
        out_specs=vmem,
        scratch_shapes=[
            pltpu.SMEM((UNITS,), jnp.int32),
            pltpu.VMEM((4, UNITS, 2, ROWS, COLS), f32),
            pltpu.VMEM((UNITS, ROWS, COLS), jnp.bfloat16),
            pltpu.VMEM((ROWS, COLS), f32),
            pltpu.VMEM((4, 8, COLS), f32),
            pltpu.VMEM((LEAD, 8, COLS), jnp.int32),
            pltpu.VMEM((KINDS * TWO, TWO), jnp.bfloat16),
            pltpu.VMEM((KINDS * TWO, TWO), jnp.bfloat16),
            pltpu.VMEM((15 * ROWS, KINDS * TWO), jnp.bfloat16),
            pltpu.VMEM((15 * ROWS, KINDS * TWO), jnp.bfloat16),
            pltpu.VMEM((15, 2, ROWS, COLS), f32),
            pltpu.VMEM((2, ROWS, COLS), f32),
        ],
    )(bond_map, bond_strength, drive_amplitude, gathered, couplings)
    back = lax.all_to_all(result, line, 0, 0, tiled=True)
    return pl.pallas_call(
        unpack_kernel,
        out_shape=jax.ShapeDtypeStruct((2, ROWS, COLS), f32),
        in_specs=[vmem],
        out_specs=vmem,
    )(back)


def solution(mesh):
    names = ("grp", "plane", "far")
    split = Mesh(mesh.devices.reshape(16, 16, 4), names)
    in_specs = (P(None, names, None), P(), P(names), P(), P(), P())
    return jax.shard_map(body, mesh=split, in_specs=in_specs, out_specs=P(None, names, None), check_vma=False)
```

```python
import functools

import jax
import jax.numpy as jnp
from jax import lax
from jax.experimental import pallas as pl
from jax.experimental.pallas import tpu as pltpu
from jax.sharding import Mesh, PartitionSpec as P

BROWS = 16
STEP_SIZE = 0.5

ROWS = 64
COLS = 128
KINDS = 12
LEAD = 10
UNITS = 16
PAYLOAD = 136
TWO = 2 * COLS

ORDER = sorted(range(UNITS), key=lambda u: (u.bit_count(), u))
PLACE = [ORDER.index(u) for u in range(UNITS)]
PLANE = {2: 0, 3: 1, 4: 2, 5: 3}
ROW_BIT = {0: 0, 1: 1, 6: 2, 7: 3, 8: 4, 9: 5}
GROUPS = (
    (0, (0, 1, 2, 3, 4)),
    (0, (5, 6, 7, 8, 9, 10)),
    (0, (11, 12, 13, 14)),
    (1, (0, 1, 2, 3, 4)),
    (1, (5, 6, 7, 8, 9, 10)),
    (2, (0, 1, 2, 3, 4)),
    (3, (0,)),
)
MOST = 6


def prep_kernel(index_ref, amp_ref, out_ref):
    out_ref[:, 0, 0:COLS] = amp_ref[0]
    out_ref[:, 0, COLS:TWO] = amp_ref[1]
    block = lax.broadcasted_iota(jnp.int32, (ROWS, COLS), 0) // BROWS
    kind = jnp.zeros((ROWS, COLS), jnp.int32)
    for q in range(ROWS // BROWS):
        kind = jnp.where(block == q, index_ref[q], kind)
    out_ref[:, 0, TWO : TWO + COLS] = kind.astype(jnp.float32)


def pack_kernel(in_ref, out_ref):
    real = in_ref[:, 0, 0:COLS]
    imag = in_ref[:, 0, COLS:TWO]
    kind = in_ref[:, 0, TWO : TWO + COLS]
    row = lax.broadcasted_iota(jnp.int32, (ROWS, COLS), 0)
    lane = lax.broadcasted_iota(jnp.int32, (ROWS, COLS), 1)
    kinds = jnp.sum(jnp.where(row == lane, kind, 0.0), axis=0, keepdims=True)
    kinds = jnp.broadcast_to(kinds, (PAYLOAD - 2 * ROWS, COLS))
    for u in range(UNITS):
        out_ref[u, 0:ROWS] = real
        out_ref[u, ROWS : 2 * ROWS] = imag
        out_ref[u, 2 * ROWS :] = kinds


def unpack_kernel(in_ref, out_ref):
    out_ref[0] = in_ref[:, 0, 0:COLS]
    out_ref[1] = in_ref[:, 0, COLS:TWO]


def flip_rows(field, bit):
    tiles = field.reshape(2 * ROWS // 8, 8, COLS)
    if bit >= 3:
        step = 1 << (bit - 3)
        pairs = tiles.reshape(2 * ROWS // (16 * step), 2, step, 8, COLS)
        return jnp.concatenate([pairs[:, 1:], pairs[:, :1]], axis=1).reshape(2 * ROWS, COLS)
    step = 1 << bit
    if bit == 2:
        return pltpu.roll(tiles, 4, 1).reshape(2 * ROWS, COLS)
    row = lax.broadcasted_iota(jnp.int32, (2 * ROWS // 8, 8, COLS), 1)
    up = pltpu.roll(tiles, 8 - step, 1)
    down = pltpu.roll(tiles, step, 1)
    return jnp.where((row & step) == 0, up, down).reshape(2 * ROWS, COLS)


def step_kernel(
    bond_ref,
    strength_ref,
    drive_ref,
    gathered_ref,
    couplings_hbm,
    out_ref,
    couplings_ref,
    copied,
    state_one,
    state_two,
    state_three,
    state_four,
    kinds,
    diag_ref,
    sign_ref,
    lane_ref,
    high_w,
    low_w,
    high_even,
    low_even,
    high_odd,
    low_odd,
    lead_even,
    lead_odd,
    total,
):
    f32 = jnp.float32
    bf16 = jnp.bfloat16
    copy = pltpu.make_async_copy(couplings_hbm, couplings_ref, copied)
    copy.start()
    own = lax.axis_index("plane")
    states = (state_one, state_two, state_three, state_four)
    sides = ((high_even, low_even, lead_even), (high_odd, low_odd, lead_odd))

    row = lax.broadcasted_iota(jnp.int32, (ROWS, COLS), 0)
    lane = lax.broadcasted_iota(jnp.int32, (ROWS, COLS), 1)

    diag = jnp.zeros((ROWS, COLS), f32)
    for a in range(LEAD):
        target = bond_ref[a]
        lane_ref[a] = jnp.bitwise_xor(lane[:8], jnp.left_shift(jnp.int32(1), target))
        sign = (1 - 2 * jnp.bitwise_and(jnp.right_shift(lane, target), 1)).astype(f32)
        sign = strength_ref[a] * sign
        if a in PLANE:
            sign_ref[PLANE[a]] = sign[:8]
        else:
            lead = (1 - 2 * jnp.bitwise_and(jnp.right_shift(row, ROW_BIT[a]), 1)).astype(f32)
            diag = diag + lead * sign
    diag_ref[...] = diag

    ones = jnp.ones((COLS, TWO), bf16)
    for u in ORDER:
        there = jnp.bitwise_xor(own, u)
        state_one[PLACE[u]] = gathered_ref[there, 0 : 2 * ROWS]
        listed = jnp.broadcast_to(gathered_ref[there, 2 * ROWS : 2 * ROWS + 1], (ROWS, COLS))
        spread = jnp.where(row == lane, listed, 0.0).astype(bf16)
        kinds[PLACE[u]] = jnp.dot(spread, ones, preferred_element_type=f32).astype(bf16)

    def split():
        def one(k, carry):
            parts = []
            for c in range(2):
                block = couplings_ref[c, k]
                high = block.astype(bf16)
                parts.append((high, (block - high.astype(f32)).astype(bf16)))
            for at, target in ((0, high_w), (1, low_w)):
                real, imag = parts[0][at], parts[1][at]
                top = pl.ds(pl.multiple_of(k * TWO, TWO), COLS)
                low = pl.ds(pl.multiple_of(k * TWO + COLS, COLS), COLS)
                target[top, :] = jnp.concatenate([real, -imag], axis=1)
                target[low, :] = jnp.concatenate([imag, real], axis=1)
            return carry

        lax.fori_loop(0, KINDS, one, 0)

    def left(section, u, i, side):
        x = states[section][PLACE[u]]
        both = jnp.concatenate([x[:ROWS], x[ROWS:]], axis=1)
        high = both.astype(bf16)
        low = (both - high.astype(f32)).astype(bf16)
        zero = jnp.zeros_like(high)
        kind = kinds[PLACE[u]]
        rows = slice(i * ROWS, (i + 1) * ROWS)
        for k in range(KINDS):
            chosen = kind == jnp.bfloat16(k)
            side[0][rows, k * TWO : (k + 1) * TWO] = jnp.where(chosen, high, zero)
            side[1][rows, k * TWO : (k + 1) * TWO] = jnp.where(chosen, low, zero)

    def lead(section, u, i, side):
        weight = jnp.zeros((8, COLS), f32)
        here = jnp.bitwise_xor(own, u)
        for bit in range(4):
            sign = (1 - 2 * jnp.bitwise_and(jnp.right_shift(here, bit), 1)).astype(f32)
            weight = weight + sign * sign_ref[bit]
        weight = diag_ref[...].reshape(8, 8, COLS) + weight[None]
        x = states[section][PLACE[u]]
        out = (jnp.concatenate([weight, weight], axis=0) * x.reshape(16, 8, COLS)).reshape(2 * ROWS, COLS)
        for a in range(LEAD):
            y = states[section][PLACE[u ^ (1 << PLANE[a])]] if a in PLANE else x
            where = jnp.broadcast_to(lane_ref[a][None], (16, 8, COLS)).reshape(2 * ROWS, COLS)
            shuffled = jnp.take_along_axis(y, where, axis=1)
            term = strength_ref[a] * shuffled + drive_ref[section, a] * y
            out = out + (term if a in PLANE else flip_rows(term, ROW_BIT[a]))
        side[2][i] = out

    def tasks(number):
        if number >= len(GROUPS):
            return []
        section, places = GROUPS[number]
        side = sides[number % 2]
        made = []
        for i, p in enumerate(places):
            made.append(functools.partial(left, section, ORDER[p], i, side))
            made.append(functools.partial(lead, section, ORDER[p], i, side))
        return made

    def combine(number, beside):
        section, places = GROUPS[number]
        high, low, leads = sides[number % 2]
        count = len(places)
        dot = functools.partial(jnp.dot, preferred_element_type=f32)
        out = None
        done = 0
        for k in range(KINDS):
            at = slice(k * TWO, (k + 1) * TWO)
            rows = slice(0, count * ROWS)
            part = dot(high[rows, at], high_w[at, :])
            out = part if out is None else out + part
            out = out + dot(low[rows, at], high_w[at, :])
            out = out + dot(high[rows, at], low_w[at, :])
            while done * KINDS < len(beside) * (k + 1):
                beside[done]()
                done += 1
        ahead = (0.5, 0.5, 1.0, 0.0)[section] * STEP_SIZE
        share = (1.0, 2.0, 2.0, 1.0)[section] * STEP_SIZE / 6.0
        for i, p in enumerate(places):
            h_real = out[i * ROWS : (i + 1) * ROWS, :COLS] + leads[i, :ROWS]
            h_imag = out[i * ROWS : (i + 1) * ROWS, COLS:] + leads[i, ROWS:]
            if section < 3:
                states[section + 1][p, :ROWS] = state_one[p, :ROWS] + ahead * h_imag
                states[section + 1][p, ROWS:] = state_one[p, ROWS:] - ahead * h_real
            if p == 0:
                so_far = state_one[0] if section == 0 else total[...]
                new_real = so_far[:ROWS] + share * h_imag
                new_imag = so_far[ROWS:] - share * h_real
                if section < 3:
                    total[:ROWS] = new_real
                    total[ROWS:] = new_imag
                else:
                    out_ref[:, 0, 0:COLS] = new_real
                    out_ref[:, 0, COLS:TWO] = new_imag

    for task in tasks(0):
        task()
    copy.wait()
    split()
    for number in range(len(GROUPS)):
        beside = tasks(number + 1)
        early = len(beside) if number < 4 else 2 if number == 4 else 0
        combine(number, beside[:early])
        for task in beside[early:]:
            task()


def body(amplitudes, couplings, block_index, bond_map, bond_strength, drive_amplitude):
    f32 = jnp.float32
    bf16 = jnp.bfloat16
    vmem = pl.BlockSpec(memory_space=pltpu.VMEM)
    smem = pl.BlockSpec(memory_space=pltpu.SMEM)
    small = pltpu.CompilerParams(vmem_limit_bytes=4 << 20)
    line = ("grp", "far")
    sent = pl.pallas_call(
        prep_kernel,
        out_shape=jax.ShapeDtypeStruct((ROWS, 1, TWO + COLS), f32),
        in_specs=[smem, vmem],
        out_specs=vmem,
        compiler_params=small,
    )(block_index, amplitudes)
    held = lax.all_to_all(sent, line, 0, 0, tiled=True)
    copies = pl.pallas_call(
        pack_kernel,
        out_shape=jax.ShapeDtypeStruct((UNITS, PAYLOAD, COLS), f32),
        in_specs=[vmem],
        out_specs=vmem,
        compiler_params=small,
    )(held)
    gathered = lax.all_to_all(copies, "plane", 0, 0, tiled=True)
    wide = KINDS * TWO
    result = pl.pallas_call(
        step_kernel,
        out_shape=jax.ShapeDtypeStruct((ROWS, 1, TWO), f32),
        in_specs=[smem, smem, smem, vmem, pl.BlockSpec(memory_space=pl.ANY)],
        out_specs=vmem,
        scratch_shapes=[
            pltpu.VMEM((2, KINDS, COLS, COLS), f32),
            pltpu.SemaphoreType.DMA,
        ]
        + [pltpu.VMEM((n, 2 * ROWS, COLS), f32) for n in (16, 15, 11, 5)]
        + [
            pltpu.VMEM((UNITS, ROWS, TWO), bf16),
            pltpu.VMEM((ROWS, COLS), f32),
            pltpu.VMEM((4, 8, COLS), f32),
            pltpu.VMEM((LEAD, 8, COLS), jnp.int32),
            pltpu.VMEM((wide, TWO), bf16),
            pltpu.VMEM((wide, TWO), bf16),
        ]
        + [pltpu.VMEM((MOST * ROWS, wide), bf16)] * 4
        + [pltpu.VMEM((MOST, 2 * ROWS, COLS), f32)] * 2
        + [pltpu.VMEM((2 * ROWS, COLS), f32)],
        compiler_params=pltpu.CompilerParams(vmem_limit_bytes=32 << 20),
    )(bond_map, bond_strength, drive_amplitude, gathered, couplings)
    back = lax.all_to_all(result, line, 0, 0, tiled=True)
    return pl.pallas_call(
        unpack_kernel,
        out_shape=jax.ShapeDtypeStruct((2, ROWS, COLS), f32),
        in_specs=[vmem],
        out_specs=vmem,
        compiler_params=small,
    )(back)


def solution(mesh):
    names = ("grp", "plane", "far")
    split = Mesh(mesh.devices.reshape(16, 16, 4), names)
    in_specs = (P(None, names, None), P(), P(names), P(), P(), P())
    return jax.shard_map(body, mesh=split, in_specs=in_specs, out_specs=P(None, names, None), check_vma=False)
```

```python
import functools
import itertools

import jax
import jax.numpy as jnp
from jax import lax
from jax.experimental import pallas as pl
from jax.experimental.pallas import tpu as pltpu
from jax.sharding import Mesh, PartitionSpec as P

BROWS = 16
STEP_SIZE = 0.5

ROWS = 64
COLS = 128
KINDS = 12
LEAD = 10
UNITS = 16
PAYLOAD = 2 * ROWS + 8
TWO = 2 * COLS

ORDER = sorted(range(UNITS), key=lambda u: (u.bit_count(), u))
PLACE = [ORDER.index(u) for u in range(UNITS)]
PLANE = {2: 0, 3: 1, 4: 2, 5: 3}
ROW_BIT = {0: 0, 1: 1, 6: 2, 7: 3, 8: 4, 9: 5}
GROUPS = (
    (0, (0, 1, 2, 3, 4, 5, 6)),
    (0, (7, 8, 9, 10, 11, 12, 13, 14)),
    (1, (0, 1, 2, 3, 4)),
    (1, (5, 6, 7, 8, 9, 10)),
    (2, (0, 1, 2, 3, 4)),
    (3, (0,)),
)
MOST = 8


def prep_kernel(index_hbm, amp_hbm, out_ref, index_ref, amp_ref, copied):
    copies = (
        pltpu.make_async_copy(amp_hbm, amp_ref, copied.at[0]),
        pltpu.make_async_copy(index_hbm, index_ref, copied.at[1]),
    )
    for copy in copies:
        copy.start()
    for copy in copies:
        copy.wait()
    out_ref[:, 0, 0:COLS] = amp_ref[0]
    out_ref[:, 0, COLS:TWO] = amp_ref[1]
    block = lax.broadcasted_iota(jnp.int32, (ROWS, COLS), 0) // BROWS
    kind = jnp.zeros((ROWS, COLS), jnp.int32)
    for q in range(ROWS // BROWS):
        kind = jnp.where(block == q, index_ref[q], kind)
    out_ref[:, 0, TWO : TWO + COLS] = kind.astype(jnp.float32)


def pack_kernel(in_ref, out_ref):
    real = in_ref[:, 0, 0:COLS]
    imag = in_ref[:, 0, COLS:TWO]
    kind = in_ref[:, 0, TWO : TWO + COLS]
    row = lax.broadcasted_iota(jnp.int32, (ROWS, COLS), 0)
    lane = lax.broadcasted_iota(jnp.int32, (ROWS, COLS), 1)
    kinds = jnp.sum(jnp.where(row == lane, kind, 0.0), axis=0, keepdims=True)
    kinds = jnp.broadcast_to(kinds, (PAYLOAD - 2 * ROWS, COLS))
    for u in range(UNITS):
        out_ref[u, 0:ROWS] = real
        out_ref[u, ROWS : 2 * ROWS] = imag
        out_ref[u, 2 * ROWS :] = kinds


def unpack_kernel(in_ref, out_ref):
    out_ref[0] = in_ref[:, 0, 0:COLS]
    out_ref[1] = in_ref[:, 0, COLS:TWO]


def flip_rows(field, bit):
    tiles = field.reshape(2 * ROWS // 8, 8, COLS)
    if bit >= 3:
        step = 1 << (bit - 3)
        pairs = tiles.reshape(2 * ROWS // (16 * step), 2, step, 8, COLS)
        return jnp.concatenate([pairs[:, 1:], pairs[:, :1]], axis=1).reshape(2 * ROWS, COLS)
    step = 1 << bit
    if bit == 2:
        return pltpu.roll(tiles, 4, 1).reshape(2 * ROWS, COLS)
    row = lax.broadcasted_iota(jnp.int32, (2 * ROWS // 8, 8, COLS), 1)
    up = pltpu.roll(tiles, 8 - step, 1)
    down = pltpu.roll(tiles, step, 1)
    return jnp.where((row & step) == 0, up, down).reshape(2 * ROWS, COLS)


def step_kernel(
    bond_ref,
    strength_ref,
    drive_ref,
    gathered_ref,
    couplings_hbm,
    out_ref,
    couplings_ref,
    copied,
    state_one,
    state_two,
    state_three,
    state_four,
    kinds,
    diag_ref,
    sign_ref,
    lane_ref,
    high_w,
    low_w,
    left_even,
    left_odd,
    lead_ref,
    total,
):
    f32 = jnp.float32
    bf16 = jnp.bfloat16
    copy = pltpu.make_async_copy(couplings_hbm, couplings_ref, copied)
    copy.start()
    own = lax.axis_index("plane")
    states = (state_one, state_two, state_three, state_four)
    sides = (left_even, left_odd)

    row = lax.broadcasted_iota(jnp.int32, (ROWS, COLS), 0)
    lane = lax.broadcasted_iota(jnp.int32, (ROWS, COLS), 1)

    diag = jnp.zeros((ROWS, COLS), f32)
    for a in range(LEAD):
        target = bond_ref[a]
        lane_ref[a] = jnp.bitwise_xor(lane[:8], jnp.left_shift(jnp.int32(1), target))
        sign = (1 - 2 * jnp.bitwise_and(jnp.right_shift(lane, target), 1)).astype(f32)
        sign = strength_ref[a] * sign
        if a in PLANE:
            sign_ref[PLANE[a]] = sign[:8]
        else:
            lead = (1 - 2 * jnp.bitwise_and(jnp.right_shift(row, ROW_BIT[a]), 1)).astype(f32)
            diag = diag + lead * sign
    diag_ref[...] = diag

    ones = jnp.ones((COLS, TWO), bf16)
    for u in ORDER:
        there = jnp.bitwise_xor(own, u)
        state_one[PLACE[u]] = gathered_ref[there, 0 : 2 * ROWS]
        listed = jnp.broadcast_to(gathered_ref[there, 2 * ROWS : 2 * ROWS + 1], (ROWS, COLS))
        spread = jnp.where(row == lane, listed, 0.0).astype(bf16)
        kinds[PLACE[u]] = jnp.dot(spread, ones, preferred_element_type=f32).astype(bf16)

    def split(k):
        parts = []
        for c in range(2):
            block = couplings_ref[c, k]
            high = block.astype(bf16)
            parts.append((high, (block - high.astype(f32)).astype(bf16)))
        for at, target in ((0, high_w), (1, low_w)):
            real, imag = parts[0][at], parts[1][at]
            target[k * TWO : k * TWO + COLS] = jnp.concatenate([real, -imag], axis=1)
            target[k * TWO + COLS : (k + 1) * TWO] = jnp.concatenate([imag, real], axis=1)

    def left(section, p, i, count, side):
        x = states[section][p]
        both = jnp.concatenate([x[:ROWS], x[ROWS:]], axis=1)
        high = both.astype(bf16)
        low = (both - high.astype(f32)).astype(bf16)
        zero = jnp.zeros_like(high)
        kind = kinds[p]
        rows = slice(i * ROWS, (i + 1) * ROWS)
        more = slice((count + i) * ROWS, (count + i + 1) * ROWS)
        for k in range(KINDS):
            chosen = kind == jnp.bfloat16(k)
            side[rows, k * TWO : (k + 1) * TWO] = jnp.where(chosen, high, zero)
            side[more, k * TWO : (k + 1) * TWO] = jnp.where(chosen, low, zero)

    def lead(section, p, i):
        u = ORDER[p]
        weight = jnp.zeros((8, COLS), f32)
        here = jnp.bitwise_xor(own, u)
        for bit in range(4):
            sign = (1 - 2 * jnp.bitwise_and(jnp.right_shift(here, bit), 1)).astype(f32)
            weight = weight + sign * sign_ref[bit]
        weight = diag_ref[...].reshape(8, 8, COLS) + weight[None]
        x = states[section][p]
        out = (jnp.concatenate([weight, weight], axis=0) * x.reshape(16, 8, COLS)).reshape(2 * ROWS, COLS)
        for a in range(LEAD):
            y = states[section][PLACE[u ^ (1 << PLANE[a])]] if a in PLANE else x
            where = jnp.broadcast_to(lane_ref[a][None], (16, 8, COLS)).reshape(2 * ROWS, COLS)
            shuffled = jnp.take_along_axis(y, where, axis=1)
            term = strength_ref[a] * shuffled + drive_ref[section, a] * y
            out = out + (term if a in PLANE else flip_rows(term, ROW_BIT[a]))
        lead_ref[i] = out

    def lefts(number):
        section, places = GROUPS[number]
        count = len(places)
        side = sides[number % 2]
        return [functools.partial(left, section, p, i, count, side) for i, p in enumerate(places)]

    def combine(number):
        section, places = GROUPS[number]
        side = sides[number % 2]
        count = len(places)
        beside = [functools.partial(lead, section, p, i) for i, p in enumerate(places)]
        if number + 1 < len(GROUPS) - 1:
            ahead = lefts(number + 1)
            beside = [t for pair in itertools.zip_longest(beside, ahead) for t in pair if t is not None]
        dot = functools.partial(jnp.dot, preferred_element_type=f32)
        half = count * ROWS
        main = extra = None
        done = 0
        for k in range(KINDS):
            at = slice(k * TWO, (k + 1) * TWO)
            if number == 0 and k + 1 < KINDS:
                split(k + 1)
            part = dot(side[0 : 2 * half, at], high_w[at, :])
            main = part if main is None else main + part
            part = dot(side[0:half, at], low_w[at, :])
            extra = part if extra is None else extra + part
            while done * KINDS < len(beside) * (k + 1):
                beside[done]()
                done += 1
        ahead = (0.5, 0.5, 1.0, 0.0)[section] * STEP_SIZE
        share = (1.0, 2.0, 2.0, 1.0)[section] * STEP_SIZE / 6.0
        for i, p in enumerate(places):
            rows = slice(i * ROWS, (i + 1) * ROWS)
            out = main[rows] + main[half + i * ROWS : half + (i + 1) * ROWS] + extra[rows]
            h_real = out[:, :COLS] + lead_ref[i, :ROWS]
            h_imag = out[:, COLS:] + lead_ref[i, ROWS:]
            if section < 3:
                states[section + 1][p, :ROWS] = state_one[p, :ROWS] + ahead * h_imag
                states[section + 1][p, ROWS:] = state_one[p, ROWS:] - ahead * h_real
            if p == 0:
                so_far = state_one[0] if section == 0 else total[...]
                new_real = so_far[:ROWS] + share * h_imag
                new_imag = so_far[ROWS:] - share * h_real
                if section < 3:
                    total[:ROWS] = new_real
                    total[ROWS:] = new_imag
                else:
                    out_ref[:, 0, 0:COLS] = new_real
                    out_ref[:, 0, COLS:TWO] = new_imag

    for task in lefts(0):
        task()
    copy.wait()
    split(0)
    for number in range(len(GROUPS)):
        combine(number)
        if number == len(GROUPS) - 2:
            for task in lefts(number + 1):
                task()


def body(amplitudes, couplings, block_index, bond_map, bond_strength, drive_amplitude):
    f32 = jnp.float32
    bf16 = jnp.bfloat16
    vmem = pl.BlockSpec(memory_space=pltpu.VMEM)
    smem = pl.BlockSpec(memory_space=pltpu.SMEM)
    small = pltpu.CompilerParams(vmem_limit_bytes=4 << 20)
    line = ("grp", "far")
    sent = pl.pallas_call(
        prep_kernel,
        out_shape=jax.ShapeDtypeStruct((ROWS, 1, TWO + COLS), f32),
        in_specs=[pl.BlockSpec(memory_space=pltpu.HBM)] * 2,
        out_specs=vmem,
        scratch_shapes=[
            pltpu.SMEM((ROWS // BROWS,), jnp.int32),
            pltpu.VMEM((2, ROWS, COLS), f32),
            pltpu.SemaphoreType.DMA((2,)),
        ],
        compiler_params=small,
    )(*(pltpu.with_memory_space_constraint(array, pltpu.HBM) for array in (block_index, amplitudes)))
    held = lax.all_to_all(sent, line, 0, 0, tiled=True)
    copies = pl.pallas_call(
        pack_kernel,
        out_shape=jax.ShapeDtypeStruct((UNITS, PAYLOAD, COLS), f32),
        in_specs=[vmem],
        out_specs=vmem,
        compiler_params=small,
    )(held)
    gathered = lax.all_to_all(copies, "plane", 0, 0, tiled=True)
    wide = KINDS * TWO
    result = pl.pallas_call(
        step_kernel,
        out_shape=jax.ShapeDtypeStruct((ROWS, 1, TWO), f32),
        in_specs=[smem, smem, smem, vmem, pl.BlockSpec(memory_space=pl.ANY)],
        out_specs=vmem,
        scratch_shapes=[
            pltpu.VMEM((2, KINDS, COLS, COLS), f32),
            pltpu.SemaphoreType.DMA,
        ]
        + [pltpu.VMEM((n, 2 * ROWS, COLS), f32) for n in (16, 15, 11, 5)]
        + [
            pltpu.VMEM((UNITS, ROWS, TWO), bf16),
            pltpu.VMEM((ROWS, COLS), f32),
            pltpu.VMEM((4, 8, COLS), f32),
            pltpu.VMEM((LEAD, 8, COLS), jnp.int32),
            pltpu.VMEM((wide, TWO), bf16),
            pltpu.VMEM((wide, TWO), bf16),
        ]
        + [pltpu.VMEM((2 * MOST * ROWS, wide), bf16)] * 2
        + [pltpu.VMEM((MOST, 2 * ROWS, COLS), f32)]
        + [pltpu.VMEM((2 * ROWS, COLS), f32)],
        compiler_params=pltpu.CompilerParams(vmem_limit_bytes=32 << 20),
    )(bond_map, bond_strength, drive_amplitude, gathered, couplings)
    back = lax.all_to_all(result, line, 0, 0, tiled=True)
    return pl.pallas_call(
        unpack_kernel,
        out_shape=jax.ShapeDtypeStruct((2, ROWS, COLS), f32),
        in_specs=[vmem],
        out_specs=vmem,
        compiler_params=small,
    )(back)


def solution(mesh):
    names = ("grp", "plane", "far")
    split = Mesh(mesh.devices.reshape(16, 16, 4), names)
    in_specs = (P(None, names, None), P(), P(names), P(), P(), P())
    return jax.shard_map(body, mesh=split, in_specs=in_specs, out_specs=P(None, names, None), check_vma=False)
```

```python
import functools
import itertools

import jax
import jax.numpy as jnp
from jax import lax
from jax.experimental import pallas as pl
from jax.experimental.pallas import tpu as pltpu
from jax.sharding import Mesh, PartitionSpec as P

BROWS = 16
STEP_SIZE = 0.5

ROWS = 64
COLS = 128
KINDS = 12
LEAD = 10
UNITS = 16
PAYLOAD = 2 * ROWS + 8
TWO = 2 * COLS

ORDER = sorted(range(UNITS), key=lambda u: (u.bit_count(), u))
PLACE = [ORDER.index(u) for u in range(UNITS)]
PLANE = {2: 0, 3: 1, 4: 2, 5: 3}
ROW_BIT = {0: 0, 1: 1, 6: 2, 7: 3, 8: 4, 9: 5}
GROUPS = (
    (0, (0, 1, 2, 3, 4, 5, 6)),
    (0, (7, 8, 9, 10, 11, 12, 13, 14)),
    (1, (0, 1, 2, 3, 4)),
    (1, (5, 6, 7, 8, 9, 10)),
    (2, (0, 1, 2, 3, 4)),
    (3, (0,)),
)
MOST = 8


def prep_kernel(index_hbm, amp_hbm, out_ref, index_ref, amp_ref, copied):
    copies = (
        pltpu.make_async_copy(amp_hbm, amp_ref, copied.at[0]),
        pltpu.make_async_copy(index_hbm, index_ref, copied.at[1]),
    )
    for copy in copies:
        copy.start()
    for copy in copies:
        copy.wait()
    out_ref[:, 0, 0:COLS] = amp_ref[0]
    out_ref[:, 0, COLS:TWO] = amp_ref[1]
    block = lax.broadcasted_iota(jnp.int32, (ROWS, COLS), 0) // BROWS
    kind = jnp.zeros((ROWS, COLS), jnp.int32)
    for q in range(ROWS // BROWS):
        kind = jnp.where(block == q, index_ref[q], kind)
    out_ref[:, 0, TWO : TWO + COLS] = kind.astype(jnp.float32)


def pack_kernel(in_ref, out_ref):
    real = in_ref[:, 0, 0:COLS]
    imag = in_ref[:, 0, COLS:TWO]
    kind = in_ref[:, 0, TWO : TWO + COLS]
    row = lax.broadcasted_iota(jnp.int32, (ROWS, COLS), 0)
    lane = lax.broadcasted_iota(jnp.int32, (ROWS, COLS), 1)
    kinds = jnp.sum(jnp.where(row == lane, kind, 0.0), axis=0, keepdims=True)
    kinds = jnp.broadcast_to(kinds, (PAYLOAD - 2 * ROWS, COLS))
    for u in range(UNITS):
        out_ref[u, 0:ROWS] = real
        out_ref[u, ROWS : 2 * ROWS] = imag
        out_ref[u, 2 * ROWS :] = kinds


def unpack_kernel(in_ref, out_ref):
    out_ref[0] = in_ref[:, 0, 0:COLS]
    out_ref[1] = in_ref[:, 0, COLS:TWO]


def flip_rows(field, bit):
    tiles = field.reshape(ROWS // 8, 8, COLS)
    if bit >= 3:
        step = 1 << (bit - 3)
        pairs = tiles.reshape(ROWS // (16 * step), 2, step, 8, COLS)
        return jnp.concatenate([pairs[:, 1:], pairs[:, :1]], axis=1).reshape(ROWS, COLS)
    step = 1 << bit
    if bit == 2:
        return pltpu.roll(tiles, 4, 1).reshape(ROWS, COLS)
    row = lax.broadcasted_iota(jnp.int32, (ROWS // 8, 8, COLS), 1)
    up = pltpu.roll(tiles, 8 - step, 1)
    down = pltpu.roll(tiles, step, 1)
    return jnp.where((row & step) == 0, up, down).reshape(ROWS, COLS)


def step_kernel(
    bond_ref,
    strength_ref,
    drive_ref,
    gathered_ref,
    couplings_hbm,
    out_ref,
    couplings_ref,
    copied,
    state_one,
    state_two,
    state_three,
    state_four,
    kinds,
    diag_ref,
    sign_ref,
    lane_ref,
    high_w,
    low_w,
    left_even,
    left_odd,
    lead_ref,
    total,
):
    f32 = jnp.float32
    bf16 = jnp.bfloat16
    copy = pltpu.make_async_copy(couplings_hbm, couplings_ref, copied)
    copy.start()
    own = lax.axis_index("plane")
    states = (state_one, state_two, state_three, state_four)
    sides = (left_even, left_odd)

    row = lax.broadcasted_iota(jnp.int32, (ROWS, COLS), 0)
    lane = lax.broadcasted_iota(jnp.int32, (ROWS, COLS), 1)

    diag = jnp.zeros((ROWS, COLS), f32)
    for a in range(LEAD):
        target = bond_ref[a]
        lane_ref[a] = jnp.bitwise_xor(lane[:8], jnp.left_shift(jnp.int32(1), target))
        sign = (1 - 2 * jnp.bitwise_and(jnp.right_shift(lane, target), 1)).astype(f32)
        sign = strength_ref[a] * sign
        if a in PLANE:
            sign_ref[PLANE[a]] = sign[:8]
        else:
            lead = (1 - 2 * jnp.bitwise_and(jnp.right_shift(row, ROW_BIT[a]), 1)).astype(f32)
            diag = diag + lead * sign
    diag_ref[...] = diag

    ones = jnp.ones((COLS, TWO), bf16)
    for u in ORDER:
        there = jnp.bitwise_xor(own, u)
        state_one[PLACE[u]] = gathered_ref[there, 0 : 2 * ROWS]

    def split(k):
        parts = []
        for c in range(2):
            block = couplings_ref[c, k]
            high = block.astype(bf16)
            parts.append((high, (block - high.astype(f32)).astype(bf16)))
        for at, target in ((0, high_w), (1, low_w)):
            real, imag = parts[0][at], parts[1][at]
            target[k * TWO : k * TWO + COLS] = jnp.concatenate([real, -imag], axis=1)
            target[k * TWO + COLS : (k + 1) * TWO] = jnp.concatenate([imag, real], axis=1)

    def left(section, p, i, count, side):
        if section == 0:
            there = jnp.bitwise_xor(own, ORDER[p])
            listed = jnp.broadcast_to(gathered_ref[there, 2 * ROWS : 2 * ROWS + 1], (ROWS, COLS))
            spread = jnp.where(row == lane, listed, 0.0).astype(bf16)
            kinds[p] = jnp.dot(spread, ones, preferred_element_type=f32).astype(bf16)
        x = states[section][p]
        both = jnp.concatenate([x[:ROWS], x[ROWS:]], axis=1)
        high = both.astype(bf16)
        low = (both - high.astype(f32)).astype(bf16)
        zero = jnp.zeros_like(high)
        kind = kinds[p]
        rows = slice(i * ROWS, (i + 1) * ROWS)
        more = slice((count + i) * ROWS, (count + i + 1) * ROWS)
        for k in range(KINDS):
            chosen = kind == jnp.bfloat16(k)
            side[rows, k * TWO : (k + 1) * TWO] = jnp.where(chosen, high, zero)
            side[more, k * TWO : (k + 1) * TWO] = jnp.where(chosen, low, zero)

    def lead(section, p, i, part):
        u = ORDER[p]
        rows = slice(part * ROWS, (part + 1) * ROWS)
        weight = jnp.zeros((8, COLS), f32)
        here = jnp.bitwise_xor(own, u)
        for bit in range(4):
            sign = (1 - 2 * jnp.bitwise_and(jnp.right_shift(here, bit), 1)).astype(f32)
            weight = weight + sign * sign_ref[bit]
        weight = (diag_ref[...].reshape(8, 8, COLS) + weight[None]).reshape(ROWS, COLS)
        x = states[section][p, rows]
        out = weight * x
        for a in range(LEAD):
            y = states[section][PLACE[u ^ (1 << PLANE[a])], rows] if a in PLANE else x
            where = jnp.broadcast_to(lane_ref[a][None], (8, 8, COLS)).reshape(ROWS, COLS)
            shuffled = jnp.take_along_axis(y, where, axis=1)
            term = strength_ref[a] * shuffled + drive_ref[section, a] * y
            out = out + (term if a in PLANE else flip_rows(term, ROW_BIT[a]))
        lead_ref[i, rows] = out

    def lefts(number):
        section, places = GROUPS[number]
        count = len(places)
        side = sides[number % 2]
        return [functools.partial(left, section, p, i, count, side) for i, p in enumerate(places)]

    def combine(number):
        section, places = GROUPS[number]
        side = sides[number % 2]
        count = len(places)
        beside = [functools.partial(lead, section, p, i, part) for i, p in enumerate(places) for part in range(2)]
        if number + 1 < len(GROUPS) - 1:
            ahead = lefts(number + 1)
            beside = [t for pair in itertools.zip_longest(beside, ahead) for t in pair if t is not None]
        dot = functools.partial(jnp.dot, preferred_element_type=f32)
        half = count * ROWS
        chains = 2 if count == 1 else 1
        main, extra = [None] * chains, [None] * chains
        done = 0
        for k in range(KINDS):
            at = slice(k * TWO, (k + 1) * TWO)
            if number == 0 and k + 1 < KINDS:
                split(k + 1)
            chain = k % chains
            part = dot(side[0 : 2 * half, at], high_w[at, :])
            main[chain] = part if main[chain] is None else main[chain] + part
            part = dot(side[0:half, at], low_w[at, :])
            extra[chain] = part if extra[chain] is None else extra[chain] + part
            while done * KINDS < len(beside) * (k + 1):
                beside[done]()
                done += 1
        ahead = (0.5, 0.5, 1.0, 0.0)[section] * STEP_SIZE
        share = (1.0, 2.0, 2.0, 1.0)[section] * STEP_SIZE / 6.0
        for i, p in enumerate(places):
            rows = slice(i * ROWS, (i + 1) * ROWS)
            more = slice(half + i * ROWS, half + (i + 1) * ROWS)
            out = sum(part[rows] + part[more] for part in main) + sum(part[rows] for part in extra)
            h_real = out[:, :COLS] + lead_ref[i, :ROWS]
            h_imag = out[:, COLS:] + lead_ref[i, ROWS:]
            if section < 3:
                states[section + 1][p, :ROWS] = state_one[p, :ROWS] + ahead * h_imag
                states[section + 1][p, ROWS:] = state_one[p, ROWS:] - ahead * h_real
            if p == 0:
                so_far = state_one[0] if section == 0 else total[...]
                new_real = so_far[:ROWS] + share * h_imag
                new_imag = so_far[ROWS:] - share * h_real
                if section < 3:
                    total[:ROWS] = new_real
                    total[ROWS:] = new_imag
                else:
                    out_ref[:, 0, 0:COLS] = new_real
                    out_ref[:, 0, COLS:TWO] = new_imag

    for task in lefts(0):
        task()
    copy.wait()
    split(0)
    for number in range(len(GROUPS)):
        combine(number)
        if number == len(GROUPS) - 2:
            for task in lefts(number + 1):
                task()


def body(amplitudes, couplings, block_index, bond_map, bond_strength, drive_amplitude):
    f32 = jnp.float32
    bf16 = jnp.bfloat16
    vmem = pl.BlockSpec(memory_space=pltpu.VMEM)
    smem = pl.BlockSpec(memory_space=pltpu.SMEM)
    small = pltpu.CompilerParams(vmem_limit_bytes=4 << 20)
    line = ("grp", "far")
    sent = pl.pallas_call(
        prep_kernel,
        out_shape=jax.ShapeDtypeStruct((ROWS, 1, TWO + COLS), f32),
        in_specs=[pl.BlockSpec(memory_space=pltpu.HBM)] * 2,
        out_specs=vmem,
        scratch_shapes=[
            pltpu.SMEM((ROWS // BROWS,), jnp.int32),
            pltpu.VMEM((2, ROWS, COLS), f32),
            pltpu.SemaphoreType.DMA((2,)),
        ],
        compiler_params=small,
    )(*(pltpu.with_memory_space_constraint(array, pltpu.HBM) for array in (block_index, amplitudes)))
    held = lax.all_to_all(sent, line, 0, 0, tiled=True)
    copies = pl.pallas_call(
        pack_kernel,
        out_shape=jax.ShapeDtypeStruct((UNITS, PAYLOAD, COLS), f32),
        in_specs=[vmem],
        out_specs=vmem,
        compiler_params=small,
    )(held)
    gathered = lax.all_to_all(copies, "plane", 0, 0, tiled=True)
    wide = KINDS * TWO
    result = pl.pallas_call(
        step_kernel,
        out_shape=jax.ShapeDtypeStruct((ROWS, 1, TWO), f32),
        in_specs=[smem, smem, smem, vmem, pl.BlockSpec(memory_space=pl.ANY)],
        out_specs=vmem,
        scratch_shapes=[
            pltpu.VMEM((2, KINDS, COLS, COLS), f32),
            pltpu.SemaphoreType.DMA,
        ]
        + [pltpu.VMEM((n, 2 * ROWS, COLS), f32) for n in (16, 15, 11, 5)]
        + [
            pltpu.VMEM((UNITS, ROWS, TWO), bf16),
            pltpu.VMEM((ROWS, COLS), f32),
            pltpu.VMEM((4, 8, COLS), f32),
            pltpu.VMEM((LEAD, 8, COLS), jnp.int32),
            pltpu.VMEM((wide, TWO), bf16),
            pltpu.VMEM((wide, TWO), bf16),
        ]
        + [pltpu.VMEM((2 * MOST * ROWS, wide), bf16)] * 2
        + [pltpu.VMEM((MOST, 2 * ROWS, COLS), f32)]
        + [pltpu.VMEM((2 * ROWS, COLS), f32)],
        compiler_params=pltpu.CompilerParams(vmem_limit_bytes=32 << 20),
    )(bond_map, bond_strength, drive_amplitude, gathered, couplings)
    back = lax.all_to_all(result, line, 0, 0, tiled=True)
    return pl.pallas_call(
        unpack_kernel,
        out_shape=jax.ShapeDtypeStruct((2, ROWS, COLS), f32),
        in_specs=[vmem],
        out_specs=vmem,
        compiler_params=small,
    )(back)


def solution(mesh):
    names = ("grp", "plane", "far")
    split = Mesh(mesh.devices.reshape(16, 16, 4), names)
    in_specs = (P(None, names, None), P(), P(names), P(), P(), P())
    return jax.shard_map(body, mesh=split, in_specs=in_specs, out_specs=P(None, names, None), check_vma=False)
```
